32 devices in a mesh: dp: 16 (over z, y, x), mp: 2 (over core).
Axes of the slice: x: 2, y: 2, z: 4, core: 2. Of those that a mesh axis runs over, the one named last changes fastest.
Arguments:
- x_input: bfloat16 [32768, 768], P(('dp', 'mp')), may hold values from -6 to 6
- gain_attn: float32 [768], replicated, may hold values from 0.1 to 1.9
- offset_attn: float32 [768], replicated, may hold values from -1.8 to 1.8
- w_qkv: bfloat16 [3, 768, 768], P(None, None, 'mp'), may hold values from -0.21875 to 0.21875
- bias_qv: float32 [2, 768], P(None, 'mp'), may hold values from -1.8 to 1.8
- band_table: float32 [12, 16, 16], P('mp'), may hold values from -4 to 4
- w_proj: bfloat16 [768, 768], P('mp'), may hold values from -0.875 to 0.875
- bias_proj: float32 [768], replicated, may hold values from -1.8 to 1.8
- scale_attn: float32 [768], replicated, may hold values from 0.5 to 1.5
- gain_mlp: float32 [768], replicated, may hold values from 0.1 to 1.9
- offset_mlp: float32 [768], replicated, may hold values from -1.8 to 1.8
- w_up: bfloat16 [768, 3072], P(None, 'mp'), may hold values from -0.21875 to 0.21875
- bias_up: float32 [3072], P('mp'), may hold values from -1.8 to 1.8
- w_down: bfloat16 [3072, 768], P('mp'), may hold values from -0.109375 to 0.109375
- bias_down: float32 [768], replicated, may hold values from -1.8 to 1.8
- scale_mlp: float32 [768], replicated, may hold values from 0.5 to 1.5
- segments: int32 [16, 2048], P('dp'), may hold values from 0 to 11, never falling along the last dimension, each value on 1 to 1024 neighbouring positions
- bands: int32 [16, 2048], P('dp'), may hold values from 0 to 15
- d_output: bfloat16 [32768, 768], P(('dp', 'mp')), may hold values from -6 to 6
Outputs:
- output: bfloat16 [32768, 768], P(('dp', 'mp'))
- grad_input: float32 [32768, 768], P(('dp', 'mp'))
- grad_gain_attn: float32 [768], replicated
- grad_offset_attn: float32 [768], replicated
- grad_w_qkv: float32 [3, 768, 768], P(None, None, 'mp')
- grad_bias_qv: float32 [2, 768], P(None, 'mp')
- grad_band_table: float32 [12, 16, 16], P('mp')
- grad_w_proj: float32 [768, 768], P('mp')
- grad_bias_proj: float32 [768], replicated
- grad_scale_attn: float32 [768], replicated
- grad_gain_mlp: float32 [768], replicated
- grad_offset_mlp: float32 [768], replicated
- grad_w_up: float32 [768, 3072], P(None, 'mp')
- grad_bias_up: float32 [3072], P('mp')
- grad_w_down: float32 [3072, 768], P('mp')
- grad_bias_down: float32 [768], replicated
- grad_scale_mlp: float32 [768], replicated
The draws below stay inside these ranges and needn't reach their ends.
Inputs may be any that keep to these rules, and one draw needn't show every extreme that they name: `segments`: in each row the ids never fall, each of the 12 ids holds 1 to 1024 patches and one holds exactly 1024; id 12 - 1 marks padding.
All inputs are finite; a program needn't handle non-finite values.
Results may differ from the reference program's by a relative error of at most 0.017.
Values may be sent and summed in bfloat16 or wider, within the bound.
A program may use at most 256 MiB of HBM per device.

```python
import math
import jax
import jax.numpy as jnp
import numpy as np
from jax import lax

D = 768
HEADS = 12
HEAD_DIM = 64
FF = 3072
NB = 16
ROW_LEN = 2048
PAGES = 12
PAGE_MOST = 1024
QBLOCK = 512
ROWS = 16
TOKENS = 32768


def touch_ends(result, own_key, smallest, high):
    longest = result.shape.index(max(result.shape))
    spots = []
    for shift in (0, 1):
        where = [jax.random.randint(jax.random.fold_in(own_key, axis), (), 0, length) for axis, length in enumerate(result.shape)]
        where[longest] = (where[longest] + shift) % result.shape[longest]
        spots.append(tuple(where))
    return result.at[spots[0]].set(smallest).at[spots[1]].set(high)


def shard_levels(own_key, extent, pieces, low, largest):
    def one(axis_at, blocks):
        draws = jax.random.uniform(jax.random.fold_in(jax.random.fold_in(own_key, 6), axis_at), (blocks,), jnp.float32, low / len(pieces), largest / len(pieces))
        return jnp.repeat(jnp.exp(draws), extent[axis_at] // blocks).reshape((-1,) + (1,) * (len(extent) - axis_at - 1))

    loudness = one(*pieces[0])
    for cut in pieces[1:]:
        loudness = loudness * one(*cut)
    return loudness


def length_profile(count, total, most, lean):
    weights = [(1 << 20) // math.isqrt(rank ** lean) + 1 for rank in range(2, count + 1)]
    rest, holding = total - most - (count - 1), [1] * (count - 1)
    while rest > 0:
        movable = [i for i in range(count - 1) if holding[i] < most]
        whole, budget = sum([weights[i] for i in movable]), rest
        for i in movable:
            extra = min(most - holding[i], max(1, budget * weights[i] // whole), rest)
            holding[i] = holding[i] + extra
            rest = rest - extra
    return np.array([most] + holding)


def ragged(stream_key, count, total, limit, lean):
    if count == 2:
        one = jax.random.randint(stream_key, (), max(1, total - limit), min(limit, total - 1) + 1)
        return jnp.stack([one, total - one])
    lengths = jnp.asarray(length_profile(count, total, limit, lean), jnp.int32)
    couples = (count - 1) // 2
    source_of, sink = lengths[1:1 + 2 * couples:2], lengths[2:2 + 2 * couples:2]
    slack = jnp.minimum(source_of - 1, limit - sink)
    moved = jax.random.randint(jax.random.fold_in(stream_key, 1), (couples,), 0, 1 << 20) % (slack + 1)
    lengths = lengths.at[1:1 + 2 * couples:2].set(source_of - moved).at[2:2 + 2 * couples:2].set(sink + moved)
    return lengths[jax.random.permutation(jax.random.fold_in(stream_key, 2), count)]


def bell_draw(rng, extent, width, limit, split=(), held_as=jnp.bfloat16):
    drawn = width * jax.random.normal(rng, extent, jnp.float32)
    if split:
        drawn = drawn * shard_levels(rng, extent, split, -0.22, 0.18)
    return jnp.clip(drawn, -limit, limit).astype(held_as)


def setup_inputs(seed: int = 0) -> dict:
    streams_of = jax.random.split(jax.random.key(seed), 20)
    return {
        "x_input": bell_draw(streams_of[0], (TOKENS, D), 1.0, 6.0, ((0, 32),)),
        "gain_attn": jnp.clip(1.0 + 0.18 * jax.random.normal(streams_of[1], (D,), jnp.float32), 0.1, 1.9),
        "offset_attn": bell_draw(streams_of[2], (D,), 0.3, 1.8, (), jnp.float32),
        "w_qkv": bell_draw(streams_of[3], (3, D, D), D ** -0.5, 0.21875, ((2, 2),)),
        "bias_qv": bell_draw(streams_of[4], (2, D), 0.3, 1.8, ((1, 2),), jnp.float32),
        "band_table": bell_draw(streams_of[5], (HEADS, NB, NB), 1.0, 4.0, ((0, 2),), jnp.float32),
        "w_proj": bell_draw(streams_of[6], (D, D), (D // 16) ** -0.5, 0.875, ((0, 2),)),
        "bias_proj": bell_draw(streams_of[7], (D,), 0.3, 1.8, (), jnp.float32),
        "scale_attn": jnp.clip(1.0 + 0.1 * jax.random.normal(streams_of[8], (D,), jnp.float32), 0.5, 1.5),
        "gain_mlp": jnp.clip(1.0 + 0.18 * jax.random.normal(streams_of[9], (D,), jnp.float32), 0.1, 1.9),
        "offset_mlp": bell_draw(streams_of[10], (D,), 0.3, 1.8, (), jnp.float32),
        "w_up": bell_draw(streams_of[11], (D, FF), D ** -0.5, 0.21875, ((1, 2),)),
        "bias_up": bell_draw(streams_of[12], (FF,), 0.3, 1.8, ((0, 2),), jnp.float32),
        "w_down": bell_draw(streams_of[13], (FF, D), FF ** -0.5, 0.109375, ((0, 2),)),
        "bias_down": bell_draw(streams_of[14], (D,), 0.3, 1.8, (), jnp.float32),
        "scale_mlp": jnp.clip(1.0 + 0.1 * jax.random.normal(streams_of[15], (D,), jnp.float32), 0.5, 1.5),
        "segments": jax.vmap(lambda own: jnp.searchsorted(jnp.cumsum(ragged(own, PAGES, ROW_LEN, PAGE_MOST, 2)), jnp.arange(ROW_LEN), side="right"))(jax.random.split(streams_of[16], ROWS)).reshape((ROWS, ROW_LEN)).astype(jnp.int32),
        "bands": touch_ends(jax.random.randint(streams_of[17], (ROWS, ROW_LEN), 0, NB), jax.random.fold_in(streams_of[17], 1), 0, NB - 1).astype(jnp.int32),
        "d_output": bell_draw(streams_of[18], (TOKENS, D), 1.0, 6.0, ((0, 32),)),
    }


@jax.custom_vjp
def low(v):
    return lax.optimization_barrier(v.astype(jnp.bfloat16)).astype(jnp.float32)

@jax.custom_vjp
def low_back(v):
    return v

def low_keep(v):
    return (low(v), None)

def low_pass(kept, grad):
    return (grad,)

def back_keep(v):
    return (v, None)

def back_low(kept, grad):
    return (low(grad),)
low.defvjp(low_keep, low_pass)
low_back.defvjp(back_keep, back_low)
highest = lax.Precision.HIGHEST
norm_eps = 1e-06
masked_score = -1000000000.0

def matmul(left, right):
    return jnp.dot(left, right, precision=highest, preferred_element_type=jnp.float32)

def layer_norm(values, norm_gain, norm_offset):
    center = values - lax.optimization_barrier(jnp.mean(values, axis=-1, keepdims=True))
    variance = lax.optimization_barrier(jnp.mean(center * center, axis=-1, keepdims=True))
    return center * lax.rsqrt(variance + norm_eps) * norm_gain + norm_offset

def gelu_tanh(values):
    return 0.5 * values * (1.0 + jnp.tanh(0.7978845608028654 * (values + 0.044715 * values * values * values)))

def one_hot(labels):
    levels = jnp.arange(NB, dtype=jnp.int32)
    return (labels[:, None] == levels[None, :]).astype(jnp.float32)

def row_forward(params, row_input, row_segments, row_bands):
    gain_attn, offset_attn, w_qkv, bias_qv, band_table, w_proj, bias_proj, scale_attn, gain_mlp, offset_mlp, w_up, bias_up, w_down, bias_down, scale_mlp = params
    valid_mask = (row_segments != PAGES - 1).astype(jnp.float32)[:, None]
    normed = low(layer_norm(row_input, gain_attn, offset_attn))
    queries = low(low_back(matmul(normed, w_qkv[0])) + bias_qv[0])
    keys = low(low_back(matmul(normed, w_qkv[1])))
    values = low(low_back(matmul(normed, w_qkv[2])) + bias_qv[1])
    keys = keys.reshape(ROW_LEN, HEADS, HEAD_DIM)
    values = values.reshape(ROW_LEN, HEADS, HEAD_DIM)
    onehot_keys = one_hot(row_bands)
    factor = 1.0 / math.sqrt(HEAD_DIM)
    blocks = ROW_LEN // QBLOCK

    def attend(inputs):
        query_block, segment_block, band_block = inputs
        raw_scores = low_back(jnp.einsum('qhd,khd->hqk', query_block, keys, precision=highest) * factor)
        partial_rows = jnp.einsum('qa,hab->hqb', one_hot(band_block), band_table, precision=highest)
        band_bias = jnp.einsum('hqb,kb->hqk', partial_rows, onehot_keys, precision=highest)
        allowed = (segment_block[:, None] == row_segments[None, :]) & (row_segments[None, :] != PAGES - 1)
        scores = jnp.where(allowed[None], raw_scores + band_bias, masked_score)
        row_max = lax.optimization_barrier(jnp.max(scores, axis=-1, keepdims=True))
        weights = jnp.exp(scores - row_max)
        probability = low(weights / lax.optimization_barrier(jnp.sum(weights, axis=-1, keepdims=True)))
        return jnp.einsum('hqk,khd->qhd', probability, values, precision=highest)
    attended = lax.map(jax.checkpoint(attend), (queries.reshape(blocks, QBLOCK, HEADS, HEAD_DIM), row_segments.reshape(blocks, QBLOCK), row_bands.reshape(blocks, QBLOCK)))
    attended = low(low_back(attended.reshape(ROW_LEN, D) * valid_mask))
    attn_out = low_back(matmul(attended, w_proj)) + bias_proj
    hidden = row_input + scale_attn * attn_out
    normed_two = low(layer_norm(hidden, gain_mlp, offset_mlp))
    activated = low(gelu_tanh(low_back(matmul(normed_two, w_up)) + bias_up))
    mlp_out = low_back(matmul(activated, w_down)) + bias_down
    return (hidden + scale_mlp * mlp_out) * valid_mask

def reference(x_input, gain_attn, offset_attn, w_qkv, bias_qv, band_table, w_proj, bias_proj, scale_attn, gain_mlp, offset_mlp, w_up, bias_up, w_down, bias_down, scale_mlp, segments, bands, d_output):
    params = tuple((element.astype(jnp.float32) for element in (gain_attn, offset_attn, w_qkv, bias_qv, band_table, w_proj, bias_proj, scale_attn, gain_mlp, offset_mlp, w_up, bias_up, w_down, bias_down, scale_mlp)))
    rows_input = x_input.astype(jnp.float32).reshape(ROWS, ROW_LEN, D)

    def forward(all_input, all_params):

        def one_row(state_carry, inputs):
            row_input, row_segments, row_bands = inputs
            return (state_carry, row_forward(all_params, row_input, row_segments, row_bands))
        state_final, results = lax.scan(jax.checkpoint(one_row), jnp.zeros((), jnp.float32), (all_input, segments, bands))
        return results
    results, pullback = jax.vjp(forward, rows_input, params)
    grad_rows, grads = pullback(d_output.astype(jnp.float32).reshape(ROWS, ROW_LEN, D))
    return (results.reshape(TOKENS, D).astype(jnp.bfloat16), grad_rows.reshape(TOKENS, D), grads[0], grads[1], grads[2], grads[3], grads[4], grads[5], grads[6], grads[7], grads[8], grads[9], grads[10], grads[11], grads[12], grads[13], grads[14])
```

```python
import functools
import jax
import jax.numpy as jnp
from jax import lax
from jax.sharding import PartitionSpec as P
from jax.experimental import pallas as pl
from jax.experimental.pallas import tpu as pltpu
PAGES = 12
BLK = 256
masked_score = -1000000000.0
f32, bf16, i32 = jnp.float32, jnp.bfloat16, jnp.int32

def nn(a, b):
    return lax.dot_general(a, b, (((1,), (0,)), ((), ())), preferred_element_type=f32)

def nt(a, b):
    return lax.dot_general(a, b, (((1,), (1,)), ((), ())), preferred_element_type=f32)

def block_ranges(segments):
    rows, length = segments.shape
    first = segments[:, ::BLK]
    last = jnp.minimum(segments[:, BLK - 1 :: BLK], PAGES - 2)
    start = jnp.sum((segments[:, None, :] < first[:, :, None]).astype(i32), -1)
    stop = jnp.sum((segments[:, None, :] <= last[:, :, None]).astype(i32), -1)
    lo = start // BLK
    hi = jnp.where(stop > start, (stop + BLK - 1) // BLK, lo)
    return lo, hi

def split3(v):
    a = v.astype(bf16)
    r = v - a.astype(f32)
    b = r.astype(bf16)
    c = (r - b.astype(f32)).astype(bf16)
    return a, b, c

def features(seg, band, nb):
    length = seg.shape[1]
    rows = lax.broadcasted_iota(i32, (16, length), 0)
    one_band = jnp.where(rows == band, 1.0, 0.0).astype(f32)
    one_seg = jnp.where(rows == seg, 1.0, 0.0).astype(f32)
    same = (rows == seg) & (rows != PAGES - 1)
    mask = jnp.where(same | (rows >= PAGES), 0.0, masked_score).astype(f32)
    return one_band, one_seg, mask

def fwd_kernel(lo_ref, hi_ref, q_ref, k_ref, v_ref, seg_ref, band_ref, tab_ref, o_ref, ot_ref, ln_ref,
               kx, qx, vx):
    length = q_ref.shape[0]
    row = pl.program_id(0)
    seg = seg_ref[...]
    band = band_ref[...]
    one_band, one_seg, mask = features(seg, band, 16)
    tail = jnp.where(lax.broadcasted_iota(i32, (16, length), 0) < 3, 1.0, 0.0).astype(f32)
    auxt = jnp.concatenate([one_band, one_band, one_seg, tail], axis=0)
    aux = jnp.concatenate([auxt, auxt], axis=0).T.astype(bf16)
    lane = lax.broadcasted_iota(i32, (length, 128), 1)
    k = k_ref[...]
    left = lane < 64
    kx[0] = jnp.where(left, k, aux)
    kx[1] = jnp.where(left, aux, k)
    qt = q_ref[...].astype(f32).T.astype(bf16)
    vt = v_ref[...].astype(f32).T.astype(bf16)
    oh = one_band.astype(bf16)
    zeros16 = jnp.zeros((16, length), bf16)
    for h in range(2):
        rows = nn(tab_ref[h], oh).astype(bf16)
        base = 64 * h
        qx[h, base : base + 64, :] = qt[base : base + 64]
        other = 64 - base
        qx[h, other : other + 32, :] = rows
        qx[h, other + 32 : other + 48, :] = mask.astype(bf16)
        qx[h, other + 48 : other + 64, :] = zeros16
        vx[h, 0:64, :] = vt[base : base + 64]
        vx[h, 64:80, :] = jnp.ones((16, length), bf16)

    def qblock(qb, _):
        qo = pl.multiple_of(qb * BLK, BLK)
        q0 = qx[0, :, pl.ds(qo, BLK)]
        q1 = qx[1, :, pl.ds(qo, BLK)]
        qs = (q0, q1)

        def kblock(kb, carry):
            ko = pl.multiple_of(kb * BLK, BLK)
            out = []
            for h in range(2):
                m, acc = carry[2 * h], carry[2 * h + 1]
                s = nn(kx[h, pl.ds(ko, BLK), :], qs[h])
                m_new = jnp.maximum(m, jnp.max(s, axis=0, keepdims=True))
                p = jnp.exp(s - m_new).astype(bf16)
                alpha = jnp.exp(m - m_new)
                acc = acc * alpha + nn(vx[h, :, pl.ds(ko, BLK)], p)
                out += [m_new, acc]
            return tuple(out)

        init = (jnp.full((1, BLK), -3e38, f32), jnp.zeros((80, BLK), f32)) * 2
        m0, a0, m1, a1 = lax.fori_loop(lo_ref[row, qb], hi_ref[row, qb], kblock, init)
        valid = seg_ref[:, pl.ds(qo, BLK)] != PAGES - 1
        outs = []
        for h, (m, a) in enumerate(((m0, a0), (m1, a1))):
            total = jnp.where(valid, a[64:65], 1.0)
            outs.append(jnp.where(valid, a[:64] / total, 0.0))
            ln_ref[h : h + 1, pl.ds(qo, BLK)] = jnp.where(valid, m + jnp.log(total), 0.0)
        ot = jnp.concatenate(outs, axis=0)
        ot_ref[:, pl.ds(qo, BLK)] = ot
        o_ref[pl.ds(qo, BLK), :] = ot.T.astype(bf16)
        return 0

    lax.fori_loop(0, length // BLK, qblock, 0)

def attend(qkv, segments, bands, tab):
    _, rows, length, width = qkv.shape
    pairs = width // 128
    lo, hi = block_ranges(segments)
    seg3 = segments.reshape(rows, 1, length)
    band3 = bands.reshape(rows, 1, length)
    part = lambda c: pl.BlockSpec((None, None, length, 128), lambda r, p, *_: (c, r, 0, p))
    rowspec = pl.BlockSpec((None, 1, length), lambda r, p, *_: (r, 0, 0))
    return pl.pallas_call(
        fwd_kernel,
        out_shape=(
            jax.ShapeDtypeStruct((rows, length, width), bf16),
            jax.ShapeDtypeStruct((rows, width, length), f32),
            jax.ShapeDtypeStruct((rows, pairs, 2, length), f32),
        ),
        grid_spec=pltpu.PrefetchScalarGridSpec(
            num_scalar_prefetch=2,
            grid=(rows, pairs),
            in_specs=[part(0), part(1), part(2), rowspec, rowspec,
                      pl.BlockSpec((2, 32, 16), lambda r, p, *_: (p, 0, 0))],
            out_specs=[
                pl.BlockSpec((None, length, 128), lambda r, p, *_: (r, 0, p)),
                pl.BlockSpec((None, 128, length), lambda r, p, *_: (r, p, 0)),
                pl.BlockSpec((None, None, 2, length), lambda r, p, *_: (r, p, 0, 0)),
            ],
            scratch_shapes=[
                pltpu.VMEM((2, length, 128), bf16),
                pltpu.VMEM((2, 128, length), bf16),
                pltpu.VMEM((2, 80, length), bf16),
            ],
        ),
        name="attend",
    )(lo, hi, qkv, qkv, qkv, seg3, band3, tab)

def bwd_kernel(lo_ref, hi_ref, q_ref, k_ref, v_ref, seg_ref, band_ref, tab_ref, do_ref, ot_ref, ln_ref,
               dqkv_ref, bias_ref, table_ref,
               kx, qx, vx, dox, kt, qm, dom, dqt):
    length = q_ref.shape[0]
    row = pl.program_id(0)
    seg = seg_ref[...]
    band = band_ref[...]
    one_band, one_seg, mask = features(seg, band, 16)
    tail = jnp.where(lax.broadcasted_iota(i32, (16, length), 0) < 3, 1.0, 0.0).astype(f32)
    auxt = jnp.concatenate([one_band, one_band, one_seg, tail], axis=0)
    aux = jnp.concatenate([auxt, auxt], axis=0).T.astype(bf16)
    lane = lax.broadcasted_iota(i32, (length, 128), 1)
    left = lane < 64
    k = k_ref[...]
    q = q_ref[...]
    v = v_ref[...]
    do = do_ref[...]
    zero = jnp.zeros_like(k)
    one = jnp.ones_like(k)
    kx[0] = jnp.where(left, k, aux)
    kx[1] = jnp.where(left, aux, k)
    vx[0] = jnp.where(left, v, jnp.where(lane < 67, one, zero))
    vx[1] = jnp.where(left, jnp.where(lane < 3, one, zero), v)
    qm[0] = jnp.where(left, q, zero)
    qm[1] = jnp.where(left, zero, q)
    dom[0] = jnp.where(left, do, zero)
    dom[1] = jnp.where(left, zero, do)
    qt = q.astype(f32).T.astype(bf16)
    ktt = k.astype(f32).T.astype(bf16)
    dot = do.astype(f32).T
    dotl = dot.astype(bf16)
    oh = one_band.astype(bf16)
    prod = dot * ot_ref[...]
    rows16 = lax.broadcasted_iota(i32, (16, length), 0)

    def pieces(vec):
        a, b, c = split3(vec)
        a, b, c = a.astype(f32), b.astype(f32), c.astype(f32)
        return jnp.where(rows16 == 0, a, jnp.where(rows16 == 1, b, jnp.where(rows16 == 2, c, 0.0))).astype(bf16)

    for h in range(2):
        base = 64 * h
        other = 64 - base
        rows = nn(tab_ref[h], oh).astype(bf16)
        qx[h, base : base + 64, :] = qt[base : base + 64]
        qx[h, other : other + 32, :] = rows
        qx[h, other + 32 : other + 48, :] = mask.astype(bf16)
        qx[h, other + 48 : other + 64, :] = pieces(-ln_ref[h : h + 1, :])
        delta = jnp.sum(prod[base : base + 64], axis=0, keepdims=True)
        dox[h, base : base + 64, :] = dotl[base : base + 64]
        dox[h, other : other + 16, :] = pieces(-delta)
        dox[h, other + 16 : other + 64, :] = jnp.zeros((48, length), bf16)
        kt[h, 0:64, :] = ktt[base : base + 64]
        kt[h, 64:80, :] = oh
    dqt[...] = jnp.zeros_like(dqt)

    def kblock(kb, bias):
        ko = pl.multiple_of(kb * BLK, BLK)
        ks = [kx[h, pl.ds(ko, BLK), :] for h in range(2)]
        vs = [vx[h, pl.ds(ko, BLK), :] for h in range(2)]
        kts = [kt[h, :, pl.ds(ko, BLK)] for h in range(2)]

        def qblock(qb, carry):
            dk, dv = carry
            qo = pl.multiple_of(qb * BLK, BLK)
            for h in range(2):
                p = jnp.exp(nn(ks[h], qx[h, :, pl.ds(qo, BLK)]))
                dp = nn(vs[h], dox[h, :, pl.ds(qo, BLK)])
                ds = (p * dp).astype(bf16)
                dv = dv + nn(p.astype(bf16), dom[h, pl.ds(qo, BLK), :])
                dk = dk + nn(ds, qm[h, pl.ds(qo, BLK), :])
                dqt[h, :, pl.ds(qo, BLK)] += nn(kts[h], ds)
            return dk, dv

        zeros = jnp.zeros((BLK, 128), f32)
        dk, dv = lax.fori_loop(lo_ref[row, kb], hi_ref[row, kb], qblock, (zeros, zeros))
        dqkv_ref[1, pl.ds(ko, BLK), :] = dk.astype(bf16)
        dqkv_ref[2, pl.ds(ko, BLK), :] = dv.astype(bf16)
        return bias + jnp.sum(dv, axis=0, keepdims=True)

    bias_v = lax.fori_loop(0, length // BLK, kblock, jnp.zeros((1, 128), f32))
    dq = (jnp.concatenate([dqt[0, 0:64, :], dqt[1, 0:64, :]], axis=0) * 0.125).T
    dqkv_ref[0] = dq.astype(bf16)
    bias_ref[0:1, :] = jnp.sum(dq, axis=0, keepdims=True)
    bias_ref[1:2, :] = bias_v
    for h in range(2):
        by = dqt[h, 64:80, :]
        hi = by.astype(bf16)
        low = (by - hi.astype(f32)).astype(bf16)
        table_ref[h] = nt(oh, hi) + nt(oh, low)

def attend_back(qkv, segments, bands, tab, d_att, ot, ln):
    _, rows, length, width = qkv.shape
    pairs = width // 128
    lo, hi = block_ranges(segments)
    seg3 = segments.reshape(rows, 1, length)
    band3 = bands.reshape(rows, 1, length)
    part = lambda c: pl.BlockSpec((None, None, length, 128), lambda r, p, *_: (c, r, 0, p))
    rowspec = pl.BlockSpec((None, 1, length), lambda r, p, *_: (r, 0, 0))
    return pl.pallas_call(
        bwd_kernel,
        out_shape=(
            jax.ShapeDtypeStruct((3, rows, length, width), bf16),
            jax.ShapeDtypeStruct((rows, 2, width), f32),
            jax.ShapeDtypeStruct((rows, 2 * pairs, 16, 16), f32),
        ),
        grid_spec=pltpu.PrefetchScalarGridSpec(
            num_scalar_prefetch=2,
            grid=(rows, pairs),
            in_specs=[part(0), part(1), part(2), rowspec, rowspec,
                      pl.BlockSpec((2, 32, 16), lambda r, p, *_: (p, 0, 0)),
                      pl.BlockSpec((None, length, 128), lambda r, p, *_: (r, 0, p)),
                      pl.BlockSpec((None, 128, length), lambda r, p, *_: (r, p, 0)),
                      pl.BlockSpec((None, None, 2, length), lambda r, p, *_: (r, p, 0, 0))],
            out_specs=[
                pl.BlockSpec((3, None, length, 128), lambda r, p, *_: (0, r, 0, p)),
                pl.BlockSpec((None, 2, 128), lambda r, p, *_: (r, 0, p)),
                pl.BlockSpec((None, 2, 16, 16), lambda r, p, *_: (r, p, 0, 0)),
            ],
            scratch_shapes=[
                pltpu.VMEM((2, length, 128), bf16),
                pltpu.VMEM((2, 128, length), bf16),
                pltpu.VMEM((2, length, 128), bf16),
                pltpu.VMEM((2, 128, length), bf16),
                pltpu.VMEM((2, 80, length), bf16),
                pltpu.VMEM((2, length, 128), bf16),
                pltpu.VMEM((2, length, 128), bf16),
                pltpu.VMEM((2, 80, length), f32),
            ],
        ),
        name="attend_back",
    )(lo, hi, qkv, qkv, qkv, seg3, band3, tab, d_att, ot, ln)

def table_rows(band_table):
    t = jnp.swapaxes(band_table, 1, 2)
    upper = lax.reduce_precision(t, 8, 7).astype(bf16)
    lower = (t - lax.reduce_precision(t, 8, 7)).astype(bf16)
    return jnp.concatenate([upper, lower], axis=1)


norm_eps = 1e-06


def gelu_tanh(values):
    return (
        0.5
        * values
        * (1.0 + jnp.tanh(0.7978845608028654 * (values + 0.044715 * values * values * values)))
    )


def norm_forward(values, norm_gain, norm_offset):
    center = values - jnp.mean(values, axis=-1, keepdims=True)
    inv_std = lax.rsqrt(jnp.mean(center * center, axis=-1, keepdims=True) + norm_eps)
    scaled = center * inv_std
    return (scaled * norm_gain + norm_offset, scaled, inv_std)


def norm_backward(d_normed, scaled, inv_std, norm_gain):
    d_scaled = d_normed * norm_gain
    mean_grad = jnp.mean(d_scaled, axis=-1, keepdims=True)
    mean_cross = jnp.mean(d_scaled * scaled, axis=-1, keepdims=True)
    d_values = inv_std * (d_scaled - mean_grad - scaled * mean_cross)
    return (d_values, jnp.sum(d_normed * scaled, axis=0), jnp.sum(d_normed, axis=0))


def mm(a, b):
    return jnp.dot(a, b, preferred_element_type=f32)


def mm_nt(a, b):
    return lax.dot_general(a, b, (((1,), (1,)), ((), ())), preferred_element_type=f32)


def mm_tn(a, b):
    return lax.dot_general(a, b, (((0,), (0,)), ((), ())), preferred_element_type=f32)


def partner(value):
    return lax.ppermute(value, "mp", [(0, 1), (1, 0)])


def swap(value, bit, count):
    return lax.ppermute(value, "dp", [(i, i ^ bit) for i in range(count)])


def scatter_sum(value, order, count, index):
    for bit in order:
        half = value.shape[0] // 2
        side = (index // bit) % 2
        send = lax.dynamic_slice_in_dim(value, (1 - side) * half, half, 0)
        keep = lax.dynamic_slice_in_dim(value, side * half, half, 0)
        value = (keep.astype(f32) + swap(send, bit, count).astype(f32)).astype(bf16)
    return value


def gather_all(value, order, count, index):
    for bit in reversed(order):
        side = (index // bit) % 2
        got = swap(value, bit, count)
        value = jnp.where(
            side == 0, jnp.concatenate([value, got], 0), jnp.concatenate([got, value], 0)
        )
    return value


def total_sum(value, count, index):
    bits = [1 << i for i in range(count.bit_length() - 1)]
    if len(bits) < 3:
        orders = [bits]
    else:
        orders = [bits, [bits[1], bits[0]] + bits[2:], bits[2:] + bits[:2]]
    size = value.shape[0] // len(orders)
    parts = []
    for i, order in enumerate(orders):
        part = scatter_sum(value[i * size : (i + 1) * size], order, count, index)
        parts.append(gather_all(part, order, count, index).astype(f32))
    return jnp.concatenate(parts, 0)


def body(
    count,
    x_input,
    gain_attn,
    offset_attn,
    w_qkv,
    bias_qv,
    band_table,
    w_proj,
    bias_proj,
    scale_attn,
    gain_mlp,
    offset_mlp,
    w_up,
    bias_up,
    w_down,
    bias_down,
    scale_mlp,
    segments,
    bands,
    d_output,
):
    local = x_input.shape[0]
    rows_here, length = segments.shape
    tokens = rows_here * length
    width = w_qkv.shape[2]
    core = lax.axis_index("mp")
    index = lax.axis_index("dp")
    here, there = core * local, (1 - core) * local

    def join(mine, other):
        return jnp.where(
            core == 0, jnp.concatenate([mine, other], 0), jnp.concatenate([other, mine], 0)
        )

    w_up_o, w_down_o, w_proj_o, bias_up_o = (
        partner(w_up),
        partner(w_down),
        partner(w_proj),
        partner(bias_up),
    )
    valid_all = (segments.reshape(tokens) != PAGES - 1).astype(f32)[:, None]
    valid = lax.dynamic_slice_in_dim(valid_all, here, local, 0)
    x_float = x_input.astype(f32)
    normed, scaled_attn, inv_attn = norm_forward(x_float, gain_attn, offset_attn)
    normed = normed.astype(bf16)
    normed_all = join(normed, partner(normed))
    projected = jnp.einsum("td,cde->cte", normed_all, w_qkv, preferred_element_type=f32)
    bias3 = jnp.stack([bias_qv[0], jnp.zeros_like(bias_qv[0]), bias_qv[1]])[:, None, :]
    factor = jnp.array([0.125, 1.0, 1.0], bf16)[:, None, None]
    qkv = ((projected + bias3).astype(bf16) * factor).reshape(3, rows_here, length, width)
    tab = table_rows(band_table)
    attended, ot, ln = attend(qkv, segments, bands, tab)
    attended = attended.reshape(tokens, width)
    att_m = lax.dynamic_slice_in_dim(attended, here, local, 0)
    att_o = partner(lax.dynamic_slice_in_dim(attended, there, local, 0))
    attn_out = mm(att_m, w_proj) + mm(att_o, w_proj_o) + bias_proj
    hidden = x_float + scale_attn * attn_out
    normed_mlp, scaled_mlp, inv_mlp = norm_forward(hidden, gain_mlp, offset_mlp)
    normed_two = normed_mlp.astype(bf16)
    d_final = d_output.astype(f32) * valid
    d_mlp = d_final * scale_mlp
    d_mlp_low = d_mlp.astype(bf16)
    mlp_out = bias_down
    d_normed_mlp = 0.0
    grads_up, grads_down, grads_bias = [], [], []
    for up, down, bias in ((w_up_o, w_down_o, bias_up_o), (w_up, w_down, bias_up)):
        pre_act = mm(normed_two, up) + bias
        activated_full, gelu_pull = jax.vjp(gelu_tanh, pre_act)
        activated = activated_full.astype(bf16)
        mlp_out = mlp_out + mm(activated, down)
        d_pre = gelu_pull(mm_nt(d_mlp_low, down))[0]
        grads_bias.append(jnp.sum(d_pre, axis=0))
        d_pre_low = d_pre.astype(bf16)
        d_normed_mlp = d_normed_mlp + mm_nt(d_pre_low, up)
        grads_down.append(mm_tn(activated, d_mlp_low))
        grads_up.append(mm_tn(normed_two, d_pre_low))
    down_sum = (grads_down[1] + partner(grads_down[0].astype(bf16)).astype(f32)).astype(bf16)
    up_sum = (grads_up[1] + partner(grads_up[0].astype(bf16)).astype(f32)).astype(bf16)
    grad_w_down = total_sum(down_sum, count, index)
    grad_w_up = total_sum(up_sum, count, index)
    grad_bias_up = grads_bias[1] + partner(grads_bias[0])
    output = ((hidden + scale_mlp * mlp_out) * valid).astype(bf16)
    grad_scale_mlp = jnp.sum(d_final * mlp_out, axis=0)
    grad_bias_down = jnp.sum(d_mlp, axis=0)
    d_from_mlp, grad_gain_mlp, grad_offset_mlp = norm_backward(
        d_normed_mlp, scaled_mlp, inv_mlp, gain_mlp
    )
    d_hidden = d_final + d_from_mlp
    grad_scale_attn = jnp.sum(d_hidden * attn_out, axis=0)
    d_attn = d_hidden * scale_attn
    grad_bias_proj = jnp.sum(d_attn, axis=0)
    d_attn_low = d_attn.astype(bf16)
    d_att_o = partner((mm_nt(d_attn_low, w_proj_o) * valid).astype(bf16))
    d_att_m = (mm_nt(d_attn_low, w_proj) * valid).astype(bf16)
    d_att = join(d_att_m, d_att_o).reshape(rows_here, length, width)
    proj_sum = (mm_tn(att_m, d_attn_low) + partner(mm_tn(att_o, d_attn_low).astype(bf16)).astype(f32)).astype(bf16)
    grad_w_proj = total_sum(proj_sum, count, index)
    dqkv, grad_bias_rows, table_rows_grad = attend_back(qkv, segments, bands, tab, d_att, ot, ln)
    dqkv = dqkv.reshape(3, tokens, width)
    grad_bias_qv = jnp.sum(grad_bias_rows, axis=0)
    table_grad = jnp.sum(table_rows_grad, axis=0)
    d_partial = jnp.einsum("cte,cde->td", dqkv, w_qkv, preferred_element_type=f32)
    d_other = partner(lax.dynamic_slice_in_dim(d_partial, there, local, 0).astype(bf16))
    d_normed_attn = lax.dynamic_slice_in_dim(d_partial, here, local, 0) + d_other.astype(f32)
    qkv_sum = jnp.einsum("td,cte->cde", normed_all, dqkv, preferred_element_type=f32)
    grad_w_qkv = total_sum(
        qkv_sum.astype(bf16).reshape(-1, width), count, index
    ).reshape(w_qkv.shape)
    d_from_attn, grad_gain_attn, grad_offset_attn = norm_backward(
        d_normed_attn, scaled_attn, inv_attn, gain_attn
    )
    grad_input = d_hidden + d_from_attn
    shared = jnp.concatenate(
        [
            grad_gain_attn,
            grad_offset_attn,
            grad_bias_proj,
            grad_scale_attn,
            grad_gain_mlp,
            grad_offset_mlp,
            grad_bias_down,
            grad_scale_mlp,
        ]
    )
    shared = shared + partner(shared)
    own = [grad_bias_up, grad_bias_qv.reshape(-1), table_grad.reshape(-1)]
    packed = jnp.concatenate([shared] + own)
    bit = 1
    while bit < count:
        packed = packed + swap(packed, bit, count)
        bit *= 2
    wide = x_input.shape[1]
    s = [packed[i * wide : (i + 1) * wide] for i in range(8)]
    at = 8 * wide
    outs = []
    for item in own:
        outs.append(packed[at : at + item.shape[0]])
        at += item.shape[0]
    return (
        output,
        grad_input,
        s[0],
        s[1],
        grad_w_qkv,
        outs[1].reshape(bias_qv.shape),
        outs[2].reshape(band_table.shape),
        grad_w_proj,
        s[2],
        s[3],
        s[4],
        s[5],
        grad_w_up,
        outs[0],
        grad_w_down,
        s[6],
        s[7],
    )


def solution(mesh):
    tokens = P(("dp", "mp"), None)
    specs = (
        tokens, P(), P(), P(None, None, "mp"), P(None, "mp"), P("mp", None, None), P("mp", None),
        P(), P(), P(), P(), P(None, "mp"), P("mp"), P("mp", None), P(), P(), P("dp", None),
        P("dp", None), tokens,
    )
    outs = (
        tokens, tokens, P(), P(), P(None, None, "mp"), P(None, "mp"), P("mp", None, None),
        P("mp", None), P(), P(), P(), P(), P(None, "mp"), P("mp"), P("mp", None), P(), P(),
    )
    return jax.shard_map(
        functools.partial(body, mesh.shape["dp"]),
        mesh=mesh,
        in_specs=specs,
        out_specs=outs,
        check_vma=False,
    )
```
